32 devices in a mesh: expert: 4 (over y, x), tensor: 2 (over core), dp: 4 (over z).
Axes of the slice: x: 2, y: 2, z: 4, core: 2. Of those that a mesh axis runs over, the one named last changes fastest.
Arguments:
- tokens: bfloat16 [2048, 3072], P(('expert', 'dp'), 'tensor'), may hold values from -6 to 6
- experts_chosen: int32 [2048, 2], P(('expert', 'dp')), may hold values from 0 to 3, all different within a row; in each aligned block of 128 rows (0 to 127, 128 to 255, ...) at most 73 rows name the same one
- route_weights: float32 [2048, 2], P(('expert', 'dp')), may hold values from 0.1 to 1
- cotangent: bfloat16 [2048, 3072], P(('expert', 'dp'), 'tensor'), may hold values from -6 to 6
- gate_weight: bfloat16 [4, 3072, 8192], P('expert', 'dp', 'tensor'), may hold values from -0.15625 to 0.15625
- up_weight: bfloat16 [4, 3072, 8192], P('expert', 'dp', 'tensor'), may hold values from -0.15625 to 0.15625
- down_weight: bfloat16 [4, 8192, 3072], P('expert', 'tensor', 'dp'), may hold values from -0.09375 to 0.09375
Outputs:
- layer_output: bfloat16 [2048, 3072], P(('expert', 'dp'), 'tensor')
- token_grad: bfloat16 [2048, 3072], P(('expert', 'dp'), 'tensor')
- route_grad: float32 [2048, 2], P(('expert', 'dp'))
The draws below stay inside these ranges and needn't reach their ends.
Inputs may be any that keep to these rules, and one draw needn't show every extreme that they name: `experts_chosen`: each row names 2 different experts. Among the 128 rows of one index of expert+dp no expert is named more than 73 times, and in some such block one expert is named exactly 73 times.
All inputs are finite; a program needn't handle non-finite values.
Results may differ from the reference program's by a relative error of at most 0.0072.
Values may be sent and summed in bfloat16 or wider, within the bound.
No kernel may reach another device: no remote copies, remote signals or barrier semaphores. Data moves between devices by JAX's collectives and lax.ppermute only.
A program may use at most 256 MiB of HBM per device.

```python
import math
from functools import partial
import jax
import jax.numpy as jnp
import numpy as np
from jax import lax

D = 3072
FF = 8192
TOP = 2
TOK_DEV = 128
EXPERTS = 4
TOKENS = 2048
CAP = 73
N_TENSOR = 2


def with_spikes(drawn, stream_key, source, target, parts, factor):
    def block_of(position):
        return (jnp.arange(drawn.shape[position]) // (drawn.shape[position] // parts)).reshape((-1,) + (1,) * (drawn.ndim - 1 - position))

    near = jax.random.permutation(stream_key, parts)[block_of(target)]
    far = (block_of(target) + parts // 2) % parts
    return jnp.where((block_of(source) == near) | (block_of(source) == far), factor * drawn, drawn)


def shard_levels(rng, extent, split, low, high):
    level, own = 1.0, jax.random.fold_in(rng, 6)
    for axis_at, parts in split:
        steps = jnp.exp(jax.random.uniform(jax.random.fold_in(own, axis_at), (parts,), jnp.float32, low / len(split), high / len(split)))
        level = level * jnp.repeat(steps, extent[axis_at] // parts).reshape([-1 if axis == axis_at else 1 for axis in range(len(extent))])
    return level


def shared_out(key, own, number, rows, number_of, top, limit, lean):
    sequence = jax.random.permutation(key, number_of)
    heavy_load, ordinary = load_shares(number_of, rows * top, limit, lean, True), load_shares(number_of, rows * top, limit, lean, False)
    places = jnp.arange(number_of)

    def named(sizes, turn):
        used = int((sizes > 0).sum())
        fixed = max(1, used // 4)
        shifted = fixed + (places - fixed + turn * (used - fixed)) % max(1, number_of - fixed)
        return jnp.zeros((number_of,), jnp.int32).at[sequence[jnp.where(places < fixed, places, shifted)]].set(jnp.asarray(sizes, jnp.int32))

    sizes = jnp.where(number % 4 == 0, named(heavy_load, number // 4), named(ordinary, number - number // 4 - 1))
    mixed = jax.random.permutation(jax.random.fold_in(own, 3), number_of)
    source_of, sink = mixed[0:number_of // 2 * 2:2], mixed[1:number_of // 2 * 2:2]
    slack = jnp.minimum(sizes[source_of] - 1, limit - sizes[sink]) // 2
    slack = jnp.where((source_of == sequence[0]) | (sink == sequence[0]) | (sizes[sink] == 0), 0, jnp.maximum(slack, 0))
    shifted = jax.random.randint(jax.random.fold_in(own, 4), (number_of // 2,), 0, 1 << 20) % (slack + 1)
    sizes = sizes.at[source_of].add(-shifted).at[sink].add(shifted)
    members = jnp.searchsorted(jnp.cumsum(sizes), jnp.arange(rows * top), side="right").astype(jnp.int32)
    listing = members.reshape(top, rows).T
    listing = listing[jax.random.permutation(jax.random.fold_in(own, 1), rows)]
    turn = jax.random.randint(jax.random.fold_in(own, 2), (rows, 1), 0, top)
    return jnp.take_along_axis(listing, (jnp.arange(top)[None, :] + turn) % top, axis=1)


def load_shares(amount, total, limit, lean, full):
    weights = [(1 << 20) // math.isqrt(standing ** lean) + 1 for standing in range(1, amount + 1)]
    largest = limit if full else min(limit, max(-(-total // amount), total * weights[0] // sum(weights)))
    least = 1 if total - largest >= amount - 1 else 0
    counts, surplus = [largest] + [least] * (amount - 1), total - largest - least * (amount - 1)
    while surplus > 0:
        candidates = [i for i in range(1, amount) if counts[i] < largest] or [i for i in range(1, amount) if counts[i] < limit]
        mass, remaining = sum([weights[i] for i in candidates]), surplus
        for i in candidates:
            extra = min(limit - counts[i], max(1, remaining * weights[i] // mass), surplus)
            counts[i] = counts[i] + extra
            surplus = surplus - extra
    return np.array(counts)


def bell_draw(own_key, dims, deviation, reach, shards=(), kind=jnp.bfloat16):
    array = deviation * jax.random.normal(own_key, dims, jnp.float32)
    if shards:
        array = array * shard_levels(own_key, dims, shards, -0.22, 0.18)
    return jnp.clip(array, -reach, reach).astype(kind)


def bell_draw_with(key, dims, deviation, limit, split, heavy, held_as=jnp.bfloat16):
    array = deviation * jax.random.normal(key, dims, jnp.float32)
    if split:
        array = array * shard_levels(key, dims, split, -0.22, 0.18)
    return jnp.clip(with_spikes(array, jax.random.fold_in(key, 3), *heavy), -limit, limit).astype(held_as)


def setup_inputs(seed: int = 0) -> dict:
    arg_keys = jax.random.split(jax.random.key(seed), 8)
    tokens = bell_draw(arg_keys[0], (TOKENS, D), 1.0, 6.0, ((0, 16), (1, 2)))
    experts_chosen_keys = jax.random.split(jax.random.fold_in(arg_keys[1], 1), TOKENS // TOK_DEV)
    experts_chosen_turns = jax.random.permutation(jax.random.fold_in(arg_keys[1], 3), TOKENS // TOK_DEV)
    experts_chosen = jax.vmap(lambda own, number: shared_out(jax.random.fold_in(arg_keys[1], 2), own, number, TOK_DEV, EXPERTS, TOP, CAP, 1))(experts_chosen_keys, experts_chosen_turns).reshape((TOKENS, TOP))
    route_weights = jnp.clip(0.1 + 0.9 * jax.random.uniform(arg_keys[2], (TOKENS, TOP), jnp.float32) ** shard_levels(arg_keys[2], (TOKENS, TOP), ((0, 16),), -0.2, 0.2), 0.1, 1.0)
    cotangent = bell_draw(arg_keys[3], (TOKENS, D), 1.0, 6.0, ((0, 16), (1, 2)))
    gate_weight = bell_draw_with(arg_keys[4], (EXPERTS, D, FF), D ** -0.5, 0.15625, ((0, 4), (1, 4), (2, 2)), (2, 1, 4, 2.0))
    up_weight = bell_draw_with(arg_keys[5], (EXPERTS, D, FF), D ** -0.5, 0.15625, ((0, 4), (1, 4), (2, 2)), (2, 1, 4, 2.0))
    down_weight = bell_draw_with(arg_keys[6], (EXPERTS, FF, D), FF ** -0.5, 0.09375, ((0, 4), (1, 2), (2, 4)), (1, 2, 4, 2.0))
    return dict(tokens=tokens, experts_chosen=experts_chosen, route_weights=route_weights, cotangent=cotangent, gate_weight=gate_weight, up_weight=up_weight, down_weight=down_weight)


def slot_targets(chosen_group, capacity):
    flat_ids = chosen_group.reshape(-1).astype(jnp.int32)
    expert_hot = (flat_ids[:, None] == jnp.arange(EXPERTS, dtype=jnp.int32)[None, :]).astype(jnp.int32)
    earlier = (jnp.cumsum(expert_hot, axis=0) - expert_hot).astype(jnp.int32)
    rank_slot = jnp.sum(earlier * expert_hot, axis=1).astype(jnp.int32)
    return (flat_ids * capacity + rank_slot).astype(jnp.int32)


def rounded_sum(partials):
    rounded = lax.optimization_barrier(partials.astype(jnp.bfloat16))
    return jnp.sum(rounded.astype(jnp.float32), axis=0).astype(jnp.bfloat16)


def expert_pass(operands):
    token_rows, grad_rows, expert_gate, expert_up, expert_down = operands
    block_width = FF // N_TENSOR
    gate_pre = jnp.dot(token_rows, expert_gate, preferred_element_type=jnp.float32)
    up_pre = jnp.dot(token_rows, expert_up, preferred_element_type=jnp.float32)
    hidden = (jax.nn.silu(gate_pre) * up_pre).astype(jnp.bfloat16)
    hidden_blocks = hidden.astype(jnp.float32).reshape(-1, N_TENSOR, block_width)
    down_blocks = expert_down.astype(jnp.float32).reshape(N_TENSOR, block_width, D)
    out_rows = rounded_sum(jnp.einsum("rnf,nfd->nrd", hidden_blocks, down_blocks))
    contract = (((1,), (1,)), ((), ()))
    hidden_grad = lax.dot_general(grad_rows, expert_down, contract, preferred_element_type=jnp.float32)
    sigmoid_gate = jax.nn.sigmoid(gate_pre)
    up_grad = (hidden_grad * jax.nn.silu(gate_pre)).astype(jnp.bfloat16)
    gate_grad = (hidden_grad * up_pre * sigmoid_gate * (1.0 + gate_pre * (1.0 - sigmoid_gate))).astype(jnp.bfloat16)
    gate_blocks = expert_gate.astype(jnp.float32).reshape(D, N_TENSOR, block_width)
    up_blocks = expert_up.astype(jnp.float32).reshape(D, N_TENSOR, block_width)
    in_parts = jnp.einsum("rnf,dnf->nrd", gate_grad.astype(jnp.float32).reshape(-1, N_TENSOR, block_width), gate_blocks)
    in_parts = in_parts + jnp.einsum("rnf,dnf->nrd", up_grad.astype(jnp.float32).reshape(-1, N_TENSOR, block_width), up_blocks)
    return out_rows, rounded_sum(in_parts)


def arrange(slot_rows, groups):
    return slot_rows.reshape(groups, EXPERTS, CAP, D).transpose(1, 0, 2, 3).reshape(EXPERTS, groups * CAP, D)


def pick_pairs(expert_rows, targets, groups):
    slot_rows = expert_rows.reshape(EXPERTS, groups, CAP, D).transpose(1, 0, 2, 3).reshape(groups, EXPERTS * CAP, D)
    chosen = jnp.take_along_axis(slot_rows, targets[:, :, None], axis=1)
    return chosen.astype(jnp.float32).reshape(TOKENS, TOP, D)


def reference(tokens, experts_chosen, route_weights, cotangent, gate_weight, up_weight, down_weight):
    groups = TOKENS // TOK_DEV
    slot_count = EXPERTS * CAP
    pair_count = TOK_DEV * TOP
    targets = jax.vmap(partial(slot_targets, capacity=CAP))(experts_chosen.reshape(groups, TOK_DEV, TOP))
    token_pairs = jnp.repeat(tokens, TOP, axis=0).reshape(groups, pair_count, D)
    grad_pairs = (jnp.repeat(cotangent, TOP, axis=0).astype(jnp.float32) * route_weights.reshape(-1, 1)).astype(jnp.bfloat16)
    grad_pairs = grad_pairs.reshape(groups, pair_count, D)
    group_index = jnp.arange(groups, dtype=jnp.int32)[:, None]
    empty = jnp.zeros((groups, slot_count, D), jnp.bfloat16)
    token_slots = arrange(empty.at[group_index, targets].set(token_pairs), groups)
    grad_slots = arrange(empty.at[group_index, targets].set(grad_pairs), groups)
    out_rows, in_rows = lax.map(expert_pass, (token_slots, grad_slots, gate_weight, up_weight, down_weight))
    out_pairs = pick_pairs(out_rows, targets, groups)
    in_pairs = pick_pairs(in_rows, targets, groups)
    layer_output = jnp.sum(route_weights[:, :, None] * out_pairs, axis=1).astype(jnp.bfloat16)
    token_grad = jnp.sum(in_pairs, axis=1).astype(jnp.bfloat16)
    route_grad = jnp.sum(cotangent.astype(jnp.float32)[:, None, :] * out_pairs, axis=2)
    return layer_output, token_grad, route_grad
```

```python
import jax
import jax.numpy as jnp
from jax import lax
from jax.sharding import PartitionSpec as P

F32 = jnp.float32
BF16 = jnp.bfloat16


def swap(value, axis, shift):
    size = lax.axis_size(axis)
    return lax.ppermute(value, axis, [(i, i ^ shift) for i in range(size)])


def resplit(shard, split_dim, size, me):
    part = shard.shape[split_dim] // size

    def chunk(index):
        return lax.dynamic_slice_in_dim(shard, index * part, part, split_dim)

    return [chunk(me)] + [swap(chunk(me ^ s), "dp", s) for s in range(1, size)]


def assemble(pieces, join_dim, me):
    own = pieces[0].shape[join_dim]
    shape = list(pieces[0].shape)
    shape[join_dim] = own * len(pieces)
    whole = jnp.zeros(shape, pieces[0].dtype)
    for s, piece in enumerate(pieces):
        whole = lax.dynamic_update_slice_in_dim(whole, piece, (me ^ s) * own, join_dim)
    return whole


def local(tokens, experts_chosen, route_weights, cotangent, gate_weight, up_weight, down_weight):
    E, T, Z = lax.axis_size("expert"), lax.axis_size("tensor"), lax.axis_size("dp")
    me_e, me_t, me_d = lax.axis_index("expert"), lax.axis_index("tensor"), lax.axis_index("dp")
    B, Fh = tokens.shape
    K = experts_chosen.shape[1]
    cap = min(B, 9 * B * K // (8 * E) + 1)
    capr = -(-Z * cap // 8) * 8
    G = Z * B
    R = E * capr

    gate_p = resplit(gate_weight[0], 1, Z, me_d)
    up_p = resplit(up_weight[0], 1, Z, me_d)
    down_in = lax.optimization_barrier((down_weight[0], gate_p[1:]))[0]
    down_p = resplit(down_in, 0, Z, me_d)

    tok_g = lax.all_gather(tokens, "dp", axis=0, tiled=True)
    cot_g = lax.all_gather(cotangent, "dp", axis=0, tiled=True)
    ids = lax.all_gather(experts_chosen, "dp", axis=0, tiled=True)
    wts = lax.all_gather(route_weights, "dp", axis=0, tiled=True)
    rel = me_e ^ jnp.arange(E, dtype=jnp.int32)
    named = ids[:, :, None] == rel[None, None, :]
    hit = jnp.any(named, axis=1)
    wtok = jnp.sum(jnp.where(named, wts[:, :, None], 0.0), axis=1)
    order = jnp.arange(G, dtype=jnp.int32)
    before = (order[None, :] < order[:, None]).astype(BF16)
    pos = jnp.dot(before, hit.astype(BF16), preferred_element_type=F32)
    pos = jnp.where(hit, pos, -1.0)
    place = pos.T[:, None, :] == jnp.arange(capr, dtype=F32)[None, :, None]
    pick = place.astype(BF16).reshape(R, G)
    wslot = jnp.sum(jnp.where(place, wtok.T[:, None, :], 0.0), axis=2).reshape(R, 1)

    x_send = jnp.dot(pick, tok_g, preferred_element_type=F32).astype(BF16).reshape(E, capr, Fh)
    c_send = jnp.dot(pick, cot_g, preferred_element_type=F32)
    g_send = (c_send * wslot).astype(BF16).reshape(E, capr, Fh)
    x_half = jnp.concatenate([x_send[0]] + [swap(x_send[s], "expert", s) for s in range(1, E)], 0)
    g_half = jnp.concatenate([g_send[0]] + [swap(g_send[s], "expert", s) for s in range(1, E)], 0)
    x = lax.all_gather(x_half, "tensor", axis=1, tiled=True)
    g = lax.all_gather(g_half, "tensor", axis=1, tiled=True)

    gate = assemble(gate_p, 0, me_d)
    up = assemble(up_p, 0, me_d)
    gate_pre = jnp.dot(x, gate, preferred_element_type=F32)
    up_pre = jnp.dot(x, up, preferred_element_type=F32)
    sig = jax.nn.sigmoid(gate_pre)
    silu = gate_pre * sig
    hidden = (silu * up_pre).astype(BF16)

    down = assemble(down_p, 1, me_d)
    contract = (((1,), (1,)), ((), ()))

    def send_back(part):
        mine = lax.psum_scatter(part.astype(BF16), "tensor", scatter_dimension=1, tiled=True)
        mine = mine.reshape(E, capr, Fh)
        return jnp.concatenate([mine[0]] + [swap(mine[s], "expert", s) for s in range(1, E)], 0)

    out_back = send_back(jnp.dot(hidden, down, preferred_element_type=F32))
    heavy = jnp.where(place, wtok.T[:, None, :], 0.0).reshape(R, G)
    heavy_hi = heavy.astype(BF16)
    heavy_lo = (heavy - heavy_hi.astype(F32)).astype(BF16)
    over_rows = (((0,), (0,)), ((), ()))

    def combine(weights, rows):
        return lax.dot_general(weights, rows, over_rows, preferred_element_type=F32)

    out_tok = combine(heavy_hi, out_back) + combine(heavy_lo, out_back)
    layer_output = lax.psum_scatter(out_tok.astype(BF16), "dp", scatter_dimension=0, tiled=True)

    hidden_grad = lax.dot_general(g, down, contract, preferred_element_type=F32)
    up_grad = (hidden_grad * silu).astype(BF16)
    gate_grad = (hidden_grad * up_pre * sig * (1.0 + gate_pre * (1.0 - sig))).astype(BF16)
    in_part = lax.dot_general(gate_grad, gate, contract, preferred_element_type=F32)
    in_part = in_part + lax.dot_general(up_grad, up, contract, preferred_element_type=F32)
    in_back = send_back(in_part)
    token_grad = lax.psum_scatter(
        combine(pick, in_back).astype(BF16), "dp", scatter_dimension=0, tiled=True
    )

    dots = jnp.sum(hidden.astype(F32) * hidden_grad, axis=1).reshape(E, capr)
    dots = jnp.stack([dots[0]] + [swap(dots[s], "expert", s) for s in range(1, E)], 0)
    by_tok = jnp.sum(jnp.where(place, dots[:, :, None], 0.0), axis=1).T
    by_tok = by_tok / jnp.where(hit, wtok, 1.0)
    pair = jnp.sum(jnp.where(named, by_tok[:, None, :], 0.0), axis=2)
    pair = lax.psum(pair, ("tensor", "dp"))
    route_grad = lax.dynamic_slice_in_dim(pair, me_d * B, B, 0)
    return layer_output, token_grad, route_grad


def solution(mesh):
    rows = P(("expert", "dp"), "tensor")
    pairs = P(("expert", "dp"), None)
    wide = P("expert", "dp", "tensor")
    in_specs = (rows, pairs, pairs, rows, wide, wide, P("expert", "tensor", "dp"))
    return jax.shard_map(
        local, mesh=mesh, in_specs=in_specs, out_specs=(rows, rows, pairs), check_vma=False
    )
```

```python
import jax
import jax.numpy as jnp
from jax import lax
from jax.experimental import pallas as pl
from jax.experimental.pallas import tpu as pltpu
from jax.sharding import PartitionSpec as P

F32 = jnp.float32
BF16 = jnp.bfloat16
ROWS = (((1,), (1,)), ((), ()))
OVER = (((0,), (0,)), ((), ()))
LIGHT = pl.CostEstimate(flops=0, bytes_accessed=0, transcendentals=0)


def swap(value, axis, shift):
    size = lax.axis_size(axis)
    return lax.ppermute(value, axis, [(i, i ^ shift) for i in range(size)])


def tie(*values):
    return lax.optimization_barrier(values)


def mm(a, b):
    return jnp.dot(a, b, preferred_element_type=F32)


def mmt(a, b):
    return lax.dot_general(a, b, ROWS, preferred_element_type=F32)


def join_body(at_ref, *refs):
    parts = len(refs) - at_ref.shape[0]
    pieces, wholes = refs[:-parts], refs[-parts:]
    for n, piece in enumerate(pieces):

        @pl.when(pl.program_id(0) == n)
        def _(piece=piece):
            rows = piece.shape[0] // len(wholes)
            for k, whole in enumerate(wholes):
                whole[...] = piece[k * rows : (k + 1) * rows]


def join(pieces, dim, places, parts):
    rows, cols = pieces[0].shape
    rows //= parts
    shape = (rows * len(pieces), cols) if dim == 0 else (rows, cols * len(pieces))
    spec = pl.BlockSpec((rows, cols), lambda n, at: (at[n], 0) if dim == 0 else (0, at[n]))
    return pl.pallas_call(
        join_body,
        grid_spec=pltpu.PrefetchScalarGridSpec(
            num_scalar_prefetch=1,
            grid=(len(pieces),),
            in_specs=[pl.BlockSpec((rows * parts, cols), lambda n, at: (0, 0))] * len(pieces),
            out_specs=[spec] * parts,
        ),
        out_shape=[jax.ShapeDtypeStruct(shape, BF16)] * parts,
        cost_estimate=LIGHT,
        compiler_params=pltpu.CompilerParams(vmem_limit_bytes=56 << 20),
        name="join",
    )(places, *pieces)


def chunk_body(at_ref, gate_ref, up_ref, out_ref):
    @pl.when(pl.program_id(0) == 0)
    def _():
        out_ref[...] = gate_ref[...]

    @pl.when(pl.program_id(0) == 1)
    def _():
        out_ref[...] = up_ref[...]


def gate_up_chunk(gate, up, index, width):
    rows = gate.shape[0]
    tile = rows // 3 if rows % 48 == 0 else rows
    steps = rows // tile
    return pl.pallas_call(
        chunk_body,
        grid_spec=pltpu.PrefetchScalarGridSpec(
            num_scalar_prefetch=1,
            grid=(2, steps),
            in_specs=[
                pl.BlockSpec((tile, width), lambda p, n, at: (jnp.where(p == 0, n, steps - 1), at[0])),
                pl.BlockSpec((tile, width), lambda p, n, at: (jnp.where(p == 0, 0, n), at[0])),
            ],
            out_specs=pl.BlockSpec((tile, width), lambda p, n, at: (p * steps + n, 0)),
        ),
        out_shape=jax.ShapeDtypeStruct((2 * rows, width), BF16),
        cost_estimate=LIGHT,
        name="gate_up_chunk",
    )(jnp.reshape(index, (1,)).astype(jnp.int32), gate, up)


def product_body(a_ref, w_ref, *rest):
    total = mm(a_ref[...], w_ref[...])
    if len(rest) == 2 and rest[0].shape[1] == 1:
        total = total * rest[0][...]
    elif len(rest) == 2:
        total = total + rest[0][...].astype(F32)
    rest[-1][...] = total.astype(BF16)


def product(a, w, first, width, extra=None, scale=None):
    height, depth = a.shape
    tile = 256
    steps = width // tile
    out_spec = pl.BlockSpec((height, tile), lambda n: (0, n))
    return pl.pallas_call(
        product_body,
        grid=(steps,),
        in_specs=[
            pl.BlockSpec((height, depth), lambda n: (0, 0)),
            pl.BlockSpec((depth, tile), lambda n: (0, first * steps + n)),
        ]
        + ([] if extra is None else [out_spec])
        + ([] if scale is None else [pl.BlockSpec((height, 1), lambda n: (0, 0))]),
        out_specs=out_spec,
        out_shape=jax.ShapeDtypeStruct((height, width), BF16),
        cost_estimate=LIGHT,
        compiler_params=pltpu.CompilerParams(vmem_limit_bytes=56 << 20),
        name="product",
    )(*([a, w] + [part for part in (extra, scale) if part is not None]))


def pair_body(a_ref, b_ref, wa_ref, wb_ref, *rest):
    total = mmt(a_ref[...], wa_ref[...]) + mmt(b_ref[...], wb_ref[...])
    if len(rest) == 2:
        total = total + rest[0][...].astype(F32)
    rest[-1][...] = total.astype(BF16)


def pair_product(a, b, wa, wb, first, width, extra=None):
    height, depth = a.shape
    tile = 256
    steps = width // tile
    row_spec = pl.BlockSpec((height, depth), lambda n: (0, 0))
    col_spec = pl.BlockSpec((tile, depth), lambda n: (first * steps + n, 0))
    out_spec = pl.BlockSpec((height, tile), lambda n: (0, n))
    ins = [a, b, wa, wb] + ([] if extra is None else [extra])
    return pl.pallas_call(
        pair_body,
        grid=(steps,),
        in_specs=[row_spec, row_spec, col_spec, col_spec] + ([] if extra is None else [out_spec]),
        out_specs=out_spec,
        out_shape=jax.ShapeDtypeStruct((height, width), BF16),
        cost_estimate=LIGHT,
        compiler_params=pltpu.CompilerParams(vmem_limit_bytes=56 << 20),
        name="pair_product",
    )(*ins)


def hidden_body(xa_ref, xb_ref, gate_ref, up_ref, hid_ref, silu_ref, fac_ref):
    half = xa_ref.shape[1]

    def pre(w_ref):
        return mm(xa_ref[...], w_ref[:half]) + mm(xb_ref[...], w_ref[half:])

    gate, up = pre(gate_ref), pre(up_ref)
    sig = jax.nn.sigmoid(gate)
    silu = gate * sig
    silu_ref[...] = silu
    hid_ref[...] = (silu * up).astype(BF16)
    fac_ref[...] = up * sig * (1.0 + gate * (1.0 - sig))


def hidden_layer(xa, xb, gate, up, height):
    R, half = xa.shape
    D, Fc = gate.shape
    tile = min(256, Fc)
    row = pl.BlockSpec((height, half), lambda r, f: (r, 0))
    col = pl.BlockSpec((D, tile), lambda r, f: (0, f))
    block = pl.BlockSpec((height, tile), lambda r, f: (r, f))
    return pl.pallas_call(
        hidden_body,
        grid=(R // height, Fc // tile),
        in_specs=[row, row, col, col],
        out_specs=[block] * 3,
        out_shape=[
            jax.ShapeDtypeStruct((R, Fc), BF16),
            jax.ShapeDtypeStruct((R, Fc), F32),
            jax.ShapeDtypeStruct((R, Fc), F32),
        ],
        cost_estimate=LIGHT,
        compiler_params=pltpu.CompilerParams(vmem_limit_bytes=48 << 20),
        name="hidden_layer",
    )(xa, xb, gate, up)


def grads_body(ga_ref, gb_ref, down_ref, silu_ref, fac_ref, hid_ref, up_ref, gate_ref, dots_ref):
    half = ga_ref.shape[1]
    hg = mmt(ga_ref[...], down_ref[:, :half]) + mmt(gb_ref[...], down_ref[:, half:])
    up_ref[...] = (hg * silu_ref[...]).astype(BF16)
    gate_ref[...] = (hg * fac_ref[...]).astype(BF16)
    prod = hg * hid_ref[...].astype(F32)
    lanes = dots_ref.shape[1]
    total = prod[:, :lanes]
    for n in range(1, prod.shape[1] // lanes):
        total = total + prod[:, n * lanes : (n + 1) * lanes]

    @pl.when(pl.program_id(1) == 0)
    def _():
        dots_ref[...] = total

    @pl.when(pl.program_id(1) > 0)
    def _():
        dots_ref[...] += total


def grads(g_a, g_b, down, silu, fac, hidden, height):
    R, Fc = hidden.shape
    half = g_a.shape[1]
    tile = min(256, Fc)
    block = pl.BlockSpec((height, tile), lambda r, f: (r, f))
    return pl.pallas_call(
        grads_body,
        grid=(R // height, Fc // tile),
        in_specs=[
            pl.BlockSpec((height, half), lambda r, f: (r, 0)),
            pl.BlockSpec((height, half), lambda r, f: (r, 0)),
            pl.BlockSpec((tile, 2 * half), lambda r, f: (f, 0)),
            block,
            block,
            block,
        ],
        out_specs=[block, block, pl.BlockSpec((height, 128), lambda r, f: (r, 0))],
        out_shape=[
            jax.ShapeDtypeStruct((R, Fc), BF16),
            jax.ShapeDtypeStruct((R, Fc), BF16),
            jax.ShapeDtypeStruct((R, 128), F32),
        ],
        cost_estimate=LIGHT,
        compiler_params=pltpu.CompilerParams(vmem_limit_bytes=56 << 20),
        name="grads",
    )(g_a, g_b, down, silu, fac, hidden)


def local(tokens, experts_chosen, route_weights, cotangent, gate_weight, up_weight, down_weight):
    E, T, Z = lax.axis_size("expert"), lax.axis_size("tensor"), lax.axis_size("dp")
    me_t, me_d = lax.axis_index("tensor"), lax.axis_index("dp")
    B, Fh = tokens.shape
    K = experts_chosen.shape[1]
    cap = min(B, 9 * B * K // (8 * E) + 1)
    capr = -(-Z * cap // 8) * 8
    G = Z * B
    R = E * capr
    Dq, Ft = gate_weight.shape[1:]
    Fc = Ft // Z
    D = Dq * Z
    two = T == 2 and Z % 2 == 0 and Fh % 256 == 0
    H = R // 2

    def place_of(q):
        if not two:
            return q
        return ((q // (Z // 2)) ^ me_t) * (Z // 2) + q % (Z // 2)

    wide = [experts_chosen.astype(F32)]
    left = route_weights
    for _ in range(3):
        wide.append(left.astype(BF16).astype(F32))
        left = left - wide[-1]
    wide = jnp.concatenate(wide, axis=1).astype(BF16)
    wide = jnp.pad(wide, ((0, 0), (0, 128 - wide.shape[1])))
    tok_g = lax.all_gather(jnp.concatenate([tokens, wide], axis=1), "dp", axis=0, tiled=True)
    cot_g = lax.all_gather(cotangent, "dp", axis=0, tiled=True)

    gate_up_p = [gate_up_chunk(gate_weight[0], up_weight[0], me_d ^ s, Fc) for s in range(Z)]
    down_p = [lax.dynamic_slice_in_dim(down_weight[0], (me_d ^ s) * Fc, Fc, 0) for s in range(Z)]
    tok_g, gate_up_p, down_p = tie(tok_g, gate_up_p, down_p)
    shifts = list(range(2, Z)) + [1]
    for s in shifts:
        gate_up_p[s] = swap(gate_up_p[s], "dp", s)
    for s in shifts:
        down_p[s], gate_up_p[s] = tie(down_p[s], gate_up_p[s])
        down_p[s] = swap(down_p[s], "dp", s)

    routing = tok_g[:, Fh:].astype(F32)
    tok_g = tok_g[:, :Fh]
    ids = routing[:, :K].astype(jnp.int32)
    wts = routing[:, K : 2 * K] + routing[:, 2 * K : 3 * K] + routing[:, 3 * K : 4 * K]
    rel = jnp.arange(E, dtype=jnp.int32)
    named = ids[:, :, None] == rel[None, None, :]
    hit = jnp.any(named, axis=1)
    wtok = jnp.sum(jnp.where(named, wts[:, :, None], 0.0), axis=1)
    order = jnp.arange(G, dtype=jnp.int32)
    before = (order[None, :] < order[:, None]).astype(BF16)
    pos = jnp.where(hit, mm(before, hit.astype(BF16)), -1.0)
    place = pos.T[:, None, :] == jnp.arange(capr, dtype=F32)[None, :, None]
    pick = place.astype(BF16).reshape(R, G)
    heavy = jnp.where(place, wtok.T[:, None, :], 0.0).reshape(R, G)
    heavy_hi = heavy.astype(BF16)
    heavy_lo = (heavy - heavy_hi.astype(F32)).astype(BF16)
    wslot = jnp.sum(heavy, axis=1, keepdims=True)

    def over_expert(rows):
        rows = rows.reshape(E, capr, -1)
        return lax.all_to_all(rows, "expert", 0, 0, tiled=True).reshape(R, -1)

    def widen(half):
        if two:
            return half, swap(half, "tensor", 1)
        full = lax.all_gather(half, "tensor", axis=1, tiled=True)
        return full[:, : D // 2], full[:, D // 2 :]

    if two:
        x_send, g_send = product(pick, tok_g, 0, Fh), product(pick, cot_g, 0, Fh, scale=wslot)
    else:
        x_send, g_send = mm(pick, tok_g).astype(BF16), (mm(pick, cot_g) * wslot).astype(BF16)
    me_e = lax.axis_index("expert")
    x_back = x_send
    for s in range(1, E):
        at = (me_e ^ s) * capr
        part = swap(lax.dynamic_slice_in_dim(x_send, at, capr, 0), "expert", s)
        x_back = lax.dynamic_update_slice_in_dim(x_back, part, at, 0)
    g_send, gate_up_p = tie(g_send, gate_up_p)
    x = widen(x_back)
    g = widen(over_expert(g_send))

    places = place_of(me_d ^ jnp.arange(Z, dtype=jnp.int32))
    gate, up = join(gate_up_p, 0, places, 2)
    hidden, silu, fac = hidden_layer(x[0], x[1], gate, up, H)
    down_p, hidden, silu, fac = lax.optimization_barrier((down_p, hidden, silu, fac))
    (down,) = join(down_p, 1, places, 1)

    def combine(weights, back):
        return lax.dot_general(weights, back, OVER, preferred_element_type=F32)

    def to_blocks(value, dtype):
        def block(s):
            return lax.dynamic_slice_in_dim(value, (me_d ^ s) * B, B, 0)

        total = block(0)
        for s in range(1, Z):
            total = total + swap(block(s).astype(dtype), "dp", s).astype(F32)
        return total

    def fold(make, whole, parts):
        if not two:
            mine = lax.psum_scatter(
                whole().astype(BF16), "tensor", scatter_dimension=1, tiled=True
            )
            return [mine]
        others = [swap(make(parts + n, parts), "tensor", 1) for n in range(parts)]
        return [make(n, parts, others[n]) for n in range(parts)]

    def make_out(first, parts, extra=None):
        return product(hidden, down, first, D // 2 // parts, extra)

    (out_mine,) = fold(make_out, lambda: mm(hidden, down), 1)
    (g_mine, g_other), out_mine = tie(g, out_mine)
    out_back = over_expert(out_mine)
    up_grad, gate_grad, dots = grads(g_mine, g_other, down, silu, fac, hidden, H)

    def make_in(first, parts, extra=None):
        return pair_product(gate_grad, up_grad, gate, up, first, D // 2 // parts, extra)

    in_mine = fold(make_in, lambda: mmt(gate_grad, gate) + mmt(up_grad, up), 2)
    dots = jnp.sum(dots, axis=1)
    if two:
        dots = dots + swap(dots, "tensor", 1)
    else:
        dots = lax.psum(dots, "tensor")
    dots = dots.reshape(E, capr)
    spare = two and capr - Z * cap >= 3 and D // 4 >= capr
    if spare:
        rows3 = []
        for _ in range(3):
            rows3.append(dots.astype(BF16))
            dots = dots - rows3[-1].astype(F32)
        rows3 = jnp.pad(jnp.stack(rows3, axis=1), ((0, 0), (0, 0), (0, D // 4 - capr)))
        last = in_mine[1].reshape(E, capr, -1)
        last = lax.dynamic_update_slice(last, rows3, (0, Z * cap, 0))
        in_mine[1] = last.reshape(R, -1)
    in_mine, out_back = tie(in_mine, out_back)
    in_back = []
    for n, part in enumerate(in_mine):
        if n:
            part, in_back[n - 1] = tie(part, in_back[n - 1])
        in_back.append(over_expert(part))
    if spare:
        dots = in_back[1].reshape(E, capr, -1)[:, Z * cap : Z * cap + 3, :capr].astype(F32)
        dots = jnp.sum(dots, axis=1)
    else:
        dots = over_expert(dots.reshape(R, 1)).reshape(E, capr)
    out_tok = (combine(heavy_hi, out_back) + combine(heavy_lo, out_back)).astype(BF16)
    layer_output = lax.psum_scatter(out_tok, "dp", scatter_dimension=0, tiled=True)
    token_grad = [to_blocks(combine(pick, p), BF16).astype(BF16) for p in in_back]
    token_grad = jnp.concatenate(token_grad, axis=1)

    by_tok = jnp.sum(jnp.where(place, dots[:, :, None], 0.0), axis=1).T
    by_tok = by_tok / jnp.where(hit, wtok, 1.0)
    pair = jnp.sum(jnp.where(named, by_tok[:, None, :], 0.0), axis=2)
    route_grad = to_blocks(pair, F32)
    return layer_output, token_grad, route_grad


def solution(mesh):
    rows = P(("expert", "dp"), "tensor")
    pairs = P(("expert", "dp"), None)
    wide = P("expert", "dp", "tensor")
    in_specs = (rows, pairs, pairs, rows, wide, wide, P("expert", "tensor", "dp"))
    return jax.shard_map(
        local, mesh=mesh, in_specs=in_specs, out_specs=(rows, rows, pairs), check_vma=False
    )
```

```python
import jax
import jax.numpy as jnp
from jax import lax
from jax.experimental import pallas as pl
from jax.experimental.pallas import tpu as pltpu
from jax.sharding import PartitionSpec as P

F32 = jnp.float32
BF16 = jnp.bfloat16
ROWS = (((1,), (1,)), ((), ()))
OVER = (((0,), (0,)), ((), ()))
LIGHT = pl.CostEstimate(flops=0, bytes_accessed=0, transcendentals=0)


def swap(value, axis, shift):
    size = lax.axis_size(axis)
    return lax.ppermute(value, axis, [(i, i ^ shift) for i in range(size)])


def tie(*values):
    return lax.optimization_barrier(values)


def mm(a, b):
    return jnp.dot(a, b, preferred_element_type=F32)


def mmt(a, b):
    return lax.dot_general(a, b, ROWS, preferred_element_type=F32)


def join_body(at_ref, *refs):
    parts = len(refs) - at_ref.shape[0]
    pieces, wholes = refs[:-parts], refs[-parts:]
    for n, piece in enumerate(pieces):

        @pl.when(pl.program_id(0) == n)
        def _(piece=piece):
            rows = piece.shape[0] // len(wholes)
            for k, whole in enumerate(wholes):
                whole[...] = piece[k * rows : (k + 1) * rows]


def join(pieces, dim, places, parts):
    rows, cols = pieces[0].shape
    rows //= parts
    shape = (rows * len(pieces), cols) if dim == 0 else (rows, cols * len(pieces))
    spec = pl.BlockSpec((rows, cols), lambda n, at: (at[n], 0) if dim == 0 else (0, at[n]))
    return pl.pallas_call(
        join_body,
        grid_spec=pltpu.PrefetchScalarGridSpec(
            num_scalar_prefetch=1,
            grid=(len(pieces),),
            in_specs=[pl.BlockSpec((rows * parts, cols), lambda n, at: (0, 0))] * len(pieces),
            out_specs=[spec] * parts,
        ),
        out_shape=[jax.ShapeDtypeStruct(shape, BF16)] * parts,
        cost_estimate=LIGHT,
        compiler_params=pltpu.CompilerParams(vmem_limit_bytes=56 << 20),
        name="join",
    )(places, *pieces)


def chunk_body(at_ref, gate_ref, up_ref, out_ref):
    @pl.when(pl.program_id(0) == 0)
    def _():
        out_ref[...] = gate_ref[...]

    @pl.when(pl.program_id(0) == 1)
    def _():
        out_ref[...] = up_ref[...]


def gate_up_chunk(gate, up, index, width):
    rows = gate.shape[0]
    tile = rows // 3 if rows % 48 == 0 else rows
    steps = rows // tile
    return pl.pallas_call(
        chunk_body,
        grid_spec=pltpu.PrefetchScalarGridSpec(
            num_scalar_prefetch=1,
            grid=(2, steps),
            in_specs=[
                pl.BlockSpec((tile, width), lambda p, n, at: (jnp.where(p == 0, n, steps - 1), at[0])),
                pl.BlockSpec((tile, width), lambda p, n, at: (jnp.where(p == 0, 0, n), at[0])),
            ],
            out_specs=pl.BlockSpec((tile, width), lambda p, n, at: (p * steps + n, 0)),
        ),
        out_shape=jax.ShapeDtypeStruct((2 * rows, width), BF16),
        cost_estimate=LIGHT,
        name="gate_up_chunk",
    )(jnp.reshape(index, (1,)).astype(jnp.int32), gate, up)


def product_body(a_ref, w_ref, *rest):
    total = mm(a_ref[...], w_ref[...])
    if len(rest) == 2 and rest[0].shape[1] == 1:
        total = total * rest[0][...]
    elif len(rest) == 2:
        total = total + rest[0][...].astype(F32)
    rest[-1][...] = total.astype(BF16)


def product(a, w, first, width, extra=None, scale=None):
    height, depth = a.shape
    tile = 256
    steps = width // tile
    out_spec = pl.BlockSpec((height, tile), lambda n: (0, n))
    return pl.pallas_call(
        product_body,
        grid=(steps,),
        in_specs=[
            pl.BlockSpec((height, depth), lambda n: (0, 0)),
            pl.BlockSpec((depth, tile), lambda n: (0, first * steps + n)),
        ]
        + ([] if extra is None else [out_spec])
        + ([] if scale is None else [pl.BlockSpec((height, 1), lambda n: (0, 0))]),
        out_specs=out_spec,
        out_shape=jax.ShapeDtypeStruct((height, width), BF16),
        cost_estimate=LIGHT,
        compiler_params=pltpu.CompilerParams(vmem_limit_bytes=56 << 20),
        name="product",
    )(*([a, w] + [part for part in (extra, scale) if part is not None]))


def pair_body(a_ref, b_ref, wa_ref, wb_ref, *rest):
    total = mmt(a_ref[...], wa_ref[...]) + mmt(b_ref[...], wb_ref[...])
    if len(rest) == 2:
        total = total + rest[0][...].astype(F32)
    rest[-1][...] = total.astype(BF16)


def pair_product(a, b, wa, wb, first, width, extra=None):
    height, depth = a.shape
    tile = 256
    steps = width // tile
    row_spec = pl.BlockSpec((height, depth), lambda n: (0, 0))
    col_spec = pl.BlockSpec((tile, depth), lambda n: (first * steps + n, 0))
    out_spec = pl.BlockSpec((height, tile), lambda n: (0, n))
    ins = [a, b, wa, wb] + ([] if extra is None else [extra])
    return pl.pallas_call(
        pair_body,
        grid=(steps,),
        in_specs=[row_spec, row_spec, col_spec, col_spec] + ([] if extra is None else [out_spec]),
        out_specs=out_spec,
        out_shape=jax.ShapeDtypeStruct((height, width), BF16),
        cost_estimate=LIGHT,
        compiler_params=pltpu.CompilerParams(vmem_limit_bytes=56 << 20),
        name="pair_product",
    )(*ins)


def hidden_body(xa_ref, xb_ref, gate_ref, up_ref, hid_ref, silu_ref, fac_ref):
    half = xa_ref.shape[1]

    def pre(w_ref):
        return mm(xa_ref[...], w_ref[:half]) + mm(xb_ref[...], w_ref[half:])

    gate, up = pre(gate_ref), pre(up_ref)
    sig = jax.nn.sigmoid(gate)
    silu = gate * sig
    silu_ref[...] = silu
    hid_ref[...] = (silu * up).astype(BF16)
    fac_ref[...] = up * sig * (1.0 + gate * (1.0 - sig))


def hidden_layer(xa, xb, gate, up, height):
    R, half = xa.shape
    D, Fc = gate.shape
    tile = min(256, Fc)
    row = pl.BlockSpec((height, half), lambda r, f: (r, 0))
    col = pl.BlockSpec((D, tile), lambda r, f: (0, f))
    block = pl.BlockSpec((height, tile), lambda r, f: (r, f))
    return pl.pallas_call(
        hidden_body,
        grid=(R // height, Fc // tile),
        in_specs=[row, row, col, col],
        out_specs=[block] * 3,
        out_shape=[
            jax.ShapeDtypeStruct((R, Fc), BF16),
            jax.ShapeDtypeStruct((R, Fc), F32),
            jax.ShapeDtypeStruct((R, Fc), F32),
        ],
        cost_estimate=LIGHT,
        compiler_params=pltpu.CompilerParams(vmem_limit_bytes=48 << 20),
        name="hidden_layer",
    )(xa, xb, gate, up)


def grads_body(ga_ref, gb_ref, down_ref, silu_ref, fac_ref, hid_ref, up_ref, gate_ref, dots_ref):
    half = ga_ref.shape[1]
    hg = mmt(ga_ref[...], down_ref[:, :half]) + mmt(gb_ref[...], down_ref[:, half:])
    up_ref[...] = (hg * silu_ref[...]).astype(BF16)
    gate_ref[...] = (hg * fac_ref[...]).astype(BF16)
    prod = hg * hid_ref[...].astype(F32)
    lanes = dots_ref.shape[1]
    total = prod[:, :lanes]
    for n in range(1, prod.shape[1] // lanes):
        total = total + prod[:, n * lanes : (n + 1) * lanes]

    @pl.when(pl.program_id(1) == 0)
    def _():
        dots_ref[...] = total

    @pl.when(pl.program_id(1) > 0)
    def _():
        dots_ref[...] += total


def grads(g_a, g_b, down, silu, fac, hidden, height):
    R, Fc = hidden.shape
    half = g_a.shape[1]
    tile = min(256, Fc)
    block = pl.BlockSpec((height, tile), lambda r, f: (r, f))
    return pl.pallas_call(
        grads_body,
        grid=(R // height, Fc // tile),
        in_specs=[
            pl.BlockSpec((height, half), lambda r, f: (r, 0)),
            pl.BlockSpec((height, half), lambda r, f: (r, 0)),
            pl.BlockSpec((tile, 2 * half), lambda r, f: (f, 0)),
            block,
            block,
            block,
        ],
        out_specs=[block, block, pl.BlockSpec((height, 128), lambda r, f: (r, 0))],
        out_shape=[
            jax.ShapeDtypeStruct((R, Fc), BF16),
            jax.ShapeDtypeStruct((R, Fc), BF16),
            jax.ShapeDtypeStruct((R, 128), F32),
        ],
        cost_estimate=LIGHT,
        compiler_params=pltpu.CompilerParams(vmem_limit_bytes=56 << 20),
        name="grads",
    )(g_a, g_b, down, silu, fac, hidden)


def local(tokens, experts_chosen, route_weights, cotangent, gate_weight, up_weight, down_weight):
    E, T, Z = lax.axis_size("expert"), lax.axis_size("tensor"), lax.axis_size("dp")
    me_t, me_d = lax.axis_index("tensor"), lax.axis_index("dp")
    B, Fh = tokens.shape
    K = experts_chosen.shape[1]
    cap = min(B, 9 * B * K // (8 * E) + 1)
    capr = -(-Z * cap // 8) * 8
    G = Z * B
    R = E * capr
    Dq, Ft = gate_weight.shape[1:]
    Fc = Ft // Z
    D = Dq * Z
    two = T == 2 and Z % 2 == 0 and Fh % 256 == 0
    H = R // 2

    def place_of(q):
        if not two:
            return q
        return ((q // (Z // 2)) ^ me_t) * (Z // 2) + q % (Z // 2)

    wide = [experts_chosen.astype(F32)]
    left = route_weights
    for _ in range(3):
        wide.append(left.astype(BF16).astype(F32))
        left = left - wide[-1]
    wide = jnp.concatenate(wide, axis=1).astype(BF16)
    wide = jnp.pad(wide, ((0, 0), (0, 128 - wide.shape[1])))
    tok_g = lax.all_gather(jnp.concatenate([tokens, wide], axis=1), "dp", axis=0, tiled=True)
    cot_g = lax.all_gather(cotangent, "dp", axis=0, tiled=True)

    gate_up_p = [gate_up_chunk(gate_weight[0], up_weight[0], me_d ^ s, Fc) for s in range(Z)]
    down_p = [lax.dynamic_slice_in_dim(down_weight[0], (me_d ^ s) * Fc, Fc, 0) for s in range(Z)]
    tok_g, gate_up_p[3:], down_p = tie(tok_g, gate_up_p[3:], down_p)
    gate_up_p[1] = swap(gate_up_p[1], "dp", 1)
    for s in range(2, Z):
        if s > 2:
            gate_up_p[s], gate_up_p[s - 1] = tie(gate_up_p[s], gate_up_p[s - 1])
        gate_up_p[s] = swap(gate_up_p[s], "dp", s)
    down_p[1], gate_up_p[1] = tie(down_p[1], gate_up_p[1])
    down_p[1] = swap(down_p[1], "dp", 1)
    for s in range(2, Z):
        if s > 2:
            down_p[s], down_p[s - 1] = tie(down_p[s], down_p[s - 1])
        else:
            down_p[s], gate_up_p = tie(down_p[s], gate_up_p)
        down_p[s] = swap(down_p[s], "dp", s)

    routing = tok_g[:, Fh:].astype(F32)
    tok_g = tok_g[:, :Fh]
    ids = routing[:, :K].astype(jnp.int32)
    wts = routing[:, K : 2 * K] + routing[:, 2 * K : 3 * K] + routing[:, 3 * K : 4 * K]
    rel = jnp.arange(E, dtype=jnp.int32)
    named = ids[:, :, None] == rel[None, None, :]
    hit = jnp.any(named, axis=1)
    wtok = jnp.sum(jnp.where(named, wts[:, :, None], 0.0), axis=1)
    order = jnp.arange(G, dtype=jnp.int32)
    before = (order[None, :] < order[:, None]).astype(BF16)
    pos = jnp.where(hit, mm(before, hit.astype(BF16)), -1.0)
    place = pos.T[:, None, :] == jnp.arange(capr, dtype=F32)[None, :, None]
    pick = place.astype(BF16).reshape(R, G)
    heavy = jnp.where(place, wtok.T[:, None, :], 0.0).reshape(R, G)
    heavy_hi = heavy.astype(BF16)
    heavy_lo = (heavy - heavy_hi.astype(F32)).astype(BF16)
    wslot = jnp.sum(heavy, axis=1, keepdims=True)

    def over_expert(rows):
        rows = rows.reshape(E, capr, -1)
        return lax.all_to_all(rows, "expert", 0, 0, tiled=True).reshape(R, -1)

    def widen(half):
        if two:
            return half, swap(half, "tensor", 1)
        full = lax.all_gather(half, "tensor", axis=1, tiled=True)
        return full[:, : D // 2], full[:, D // 2 :]

    if two:
        x_send, g_send = product(pick, tok_g, 0, Fh), product(pick, cot_g, 0, Fh, scale=wslot)
    else:
        x_send, g_send = mm(pick, tok_g).astype(BF16), (mm(pick, cot_g) * wslot).astype(BF16)
    me_e = lax.axis_index("expert")
    x_back = x_send
    for s in range(1, E):
        at = (me_e ^ s) * capr
        part = swap(lax.dynamic_slice_in_dim(x_send, at, capr, 0), "expert", s)
        x_back = lax.dynamic_update_slice_in_dim(x_back, part, at, 0)
    g_send, gate_up_p = tie(g_send, gate_up_p)
    x = widen(x_back)
    g = widen(over_expert(g_send))

    places = place_of(me_d ^ jnp.arange(Z, dtype=jnp.int32))
    gate, up = join(gate_up_p, 0, places, 2)
    hidden, silu, fac = hidden_layer(x[0], x[1], gate, up, H)
    down_p, hidden, silu, fac = lax.optimization_barrier((down_p, hidden, silu, fac))
    (down,) = join(down_p, 1, places, 1)

    def combine(weights, back):
        return lax.dot_general(weights, back, OVER, preferred_element_type=F32)

    def to_blocks(value, dtype):
        def block(s):
            return lax.dynamic_slice_in_dim(value, (me_d ^ s) * B, B, 0)

        total = block(0)
        for s in range(1, Z):
            total = total + swap(block(s).astype(dtype), "dp", s).astype(F32)
        return total

    def fold(make, whole, parts):
        if not two:
            mine = lax.psum_scatter(
                whole().astype(BF16), "tensor", scatter_dimension=1, tiled=True
            )
            return [mine]
        others = [swap(make(parts + n, parts), "tensor", 1) for n in range(parts)]
        return [make(n, parts, others[n]) for n in range(parts)]

    def make_out(first, parts, extra=None):
        return product(hidden, down, first, D // 2 // parts, extra)

    (out_mine,) = fold(make_out, lambda: mm(hidden, down), 1)
    (g_mine, g_other), out_mine = tie(g, out_mine)
    out_back = over_expert(out_mine)
    up_grad, gate_grad, dots = grads(g_mine, g_other, down, silu, fac, hidden, H)

    def make_in(first, parts, extra=None):
        return pair_product(gate_grad, up_grad, gate, up, first, D // 2 // parts, extra)

    in_mine = fold(make_in, lambda: mmt(gate_grad, gate) + mmt(up_grad, up), 2)
    dots = jnp.sum(dots, axis=1)
    if two:
        dots = dots + swap(dots, "tensor", 1)
    else:
        dots = lax.psum(dots, "tensor")
    dots = dots.reshape(E, capr)
    spare = two and capr - Z * cap >= 3 and D // 4 >= capr
    if spare:
        rows3 = []
        for _ in range(3):
            rows3.append(dots.astype(BF16))
            dots = dots - rows3[-1].astype(F32)
        rows3 = jnp.pad(jnp.stack(rows3, axis=1), ((0, 0), (0, 0), (0, D // 4 - capr)))
        last = in_mine[1].reshape(E, capr, -1)
        last = lax.dynamic_update_slice(last, rows3, (0, Z * cap, 0))
        in_mine[1] = last.reshape(R, -1)
    in_mine, out_back = tie(in_mine, out_back)
    out_tok = (combine(heavy_hi, out_back) + combine(heavy_lo, out_back)).astype(BF16)
    in_back = []
    for n, part in enumerate(in_mine):
        if n:
            part, in_back[n - 1], out_tok = tie(part, in_back[n - 1], out_tok)
        in_back.append(over_expert(part))
    if spare:
        dots = in_back[1].reshape(E, capr, -1)[:, Z * cap : Z * cap + 3, :capr].astype(F32)
        dots = jnp.sum(dots, axis=1)
    else:
        dots = over_expert(dots.reshape(R, 1)).reshape(E, capr)
    layer_output = lax.psum_scatter(out_tok, "dp", scatter_dimension=0, tiled=True)
    token_grad = [to_blocks(combine(pick, p), BF16).astype(BF16) for p in in_back]
    token_grad = jnp.concatenate(token_grad, axis=1)

    by_tok = jnp.sum(jnp.where(place, dots[:, :, None], 0.0), axis=1).T
    by_tok = by_tok / jnp.where(hit, wtok, 1.0)
    pair = jnp.sum(jnp.where(named, by_tok[:, None, :], 0.0), axis=2)
    route_grad = to_blocks(pair, F32)
    return layer_output, token_grad, route_grad


def solution(mesh):
    rows = P(("expert", "dp"), "tensor")
    pairs = P(("expert", "dp"), None)
    wide = P("expert", "dp", "tensor")
    in_specs = (rows, pairs, pairs, rows, wide, wide, P("expert", "tensor", "dp"))
    return jax.shard_map(
        local, mesh=mesh, in_specs=in_specs, out_specs=(rows, rows, pairs), check_vma=False
    )
```

```python
import jax
import jax.numpy as jnp
from jax import lax
from jax.experimental import pallas as pl
from jax.experimental.pallas import tpu as pltpu
from jax.sharding import PartitionSpec as P

F32 = jnp.float32
BF16 = jnp.bfloat16
ROWS = (((1,), (1,)), ((), ()))
OVER = (((0,), (0,)), ((), ()))
LIGHT = pl.CostEstimate(flops=0, bytes_accessed=0, transcendentals=0)


def swap(value, axis, shift):
    size = lax.axis_size(axis)
    return lax.ppermute(value, axis, [(i, i ^ shift) for i in range(size)])


def tie(*values):
    return lax.optimization_barrier(values)


def mm(a, b):
    return jnp.dot(a, b, preferred_element_type=F32)


def mmt(a, b):
    return lax.dot_general(a, b, ROWS, preferred_element_type=F32)


def join_body(at_ref, *refs):
    parts = len(refs) - at_ref.shape[0]
    pieces, wholes = refs[:-parts], refs[-parts:]
    for n, piece in enumerate(pieces):

        @pl.when(pl.program_id(0) == n)
        def _(piece=piece):
            rows = piece.shape[0] // len(wholes)
            for k, whole in enumerate(wholes):
                whole[...] = piece[k * rows : (k + 1) * rows]


def join(pieces, dim, places, parts):
    rows, cols = pieces[0].shape
    rows //= parts
    shape = (rows * len(pieces), cols) if dim == 0 else (rows, cols * len(pieces))
    spec = pl.BlockSpec((rows, cols), lambda n, at: (at[n], 0) if dim == 0 else (0, at[n]))
    return pl.pallas_call(
        join_body,
        grid_spec=pltpu.PrefetchScalarGridSpec(
            num_scalar_prefetch=1,
            grid=(len(pieces),),
            in_specs=[pl.BlockSpec((rows * parts, cols), lambda n, at: (0, 0))] * len(pieces),
            out_specs=[spec] * parts,
        ),
        out_shape=[jax.ShapeDtypeStruct(shape, BF16)] * parts,
        cost_estimate=LIGHT,
        compiler_params=pltpu.CompilerParams(vmem_limit_bytes=56 << 20),
        name="join",
    )(places, *pieces)


def chunk_body(at_ref, gate_ref, up_ref, out_ref):
    @pl.when(pl.program_id(0) == 0)
    def _():
        out_ref[...] = gate_ref[...]

    @pl.when(pl.program_id(0) == 1)
    def _():
        out_ref[...] = up_ref[...]


def gate_up_chunk(gate, up, index, width):
    rows = gate.shape[0]
    tile = rows // 3 if rows % 48 == 0 else rows
    steps = rows // tile
    return pl.pallas_call(
        chunk_body,
        grid_spec=pltpu.PrefetchScalarGridSpec(
            num_scalar_prefetch=1,
            grid=(2, steps),
            in_specs=[
                pl.BlockSpec((tile, width), lambda p, n, at: (jnp.where(p == 0, n, steps - 1), at[0])),
                pl.BlockSpec((tile, width), lambda p, n, at: (jnp.where(p == 0, 0, n), at[0])),
            ],
            out_specs=pl.BlockSpec((tile, width), lambda p, n, at: (p * steps + n, 0)),
        ),
        out_shape=jax.ShapeDtypeStruct((2 * rows, width), BF16),
        cost_estimate=LIGHT,
        name="gate_up_chunk",
    )(jnp.reshape(index, (1,)).astype(jnp.int32), gate, up)


def product_body(a_ref, w_ref, *rest):
    total = mm(a_ref[...], w_ref[...])
    if len(rest) == 2 and rest[0].shape[1] == 1:
        total = total * rest[0][...]
    elif len(rest) == 2:
        total = total + rest[0][...].astype(F32)
    rest[-1][...] = total.astype(BF16)


def product(a, w, first, width, extra=None, scale=None):
    height, depth = a.shape
    tile = 256
    steps = width // tile
    out_spec = pl.BlockSpec((height, tile), lambda n: (0, n))
    return pl.pallas_call(
        product_body,
        grid=(steps,),
        in_specs=[
            pl.BlockSpec((height, depth), lambda n: (0, 0)),
            pl.BlockSpec((depth, tile), lambda n: (0, first * steps + n)),
        ]
        + ([] if extra is None else [out_spec])
        + ([] if scale is None else [pl.BlockSpec((height, 1), lambda n: (0, 0))]),
        out_specs=out_spec,
        out_shape=jax.ShapeDtypeStruct((height, width), BF16),
        cost_estimate=LIGHT,
        compiler_params=pltpu.CompilerParams(vmem_limit_bytes=56 << 20),
        name="product",
    )(*([a, w] + [part for part in (extra, scale) if part is not None]))


def pair_body(a_ref, b_ref, wa_ref, wb_ref, *rest):
    total = mmt(a_ref[...], wa_ref[...]) + mmt(b_ref[...], wb_ref[...])
    if len(rest) == 2:
        total = total + rest[0][...].astype(F32)
    rest[-1][...] = total.astype(BF16)


def pair_product(a, b, wa, wb, first, width, extra=None):
    height, depth = a.shape
    tile = 256
    steps = width // tile
    row_spec = pl.BlockSpec((height, depth), lambda n: (0, 0))
    col_spec = pl.BlockSpec((tile, depth), lambda n: (first * steps + n, 0))
    out_spec = pl.BlockSpec((height, tile), lambda n: (0, n))
    ins = [a, b, wa, wb] + ([] if extra is None else [extra])
    return pl.pallas_call(
        pair_body,
        grid=(steps,),
        in_specs=[row_spec, row_spec, col_spec, col_spec] + ([] if extra is None else [out_spec]),
        out_specs=out_spec,
        out_shape=jax.ShapeDtypeStruct((height, width), BF16),
        cost_estimate=LIGHT,
        compiler_params=pltpu.CompilerParams(vmem_limit_bytes=56 << 20),
        name="pair_product",
    )(*ins)


def hidden_body(xa_ref, xb_ref, gate_ref, up_ref, hid_ref, silu_ref, fac_ref):
    half = xa_ref.shape[1]

    def pre(w_ref):
        return mm(xa_ref[...], w_ref[:half]) + mm(xb_ref[...], w_ref[half:])

    gate, up = pre(gate_ref), pre(up_ref)
    sig = jax.nn.sigmoid(gate)
    silu = gate * sig
    silu_ref[...] = silu
    hid_ref[...] = (silu * up).astype(BF16)
    fac_ref[...] = up * sig * (1.0 + gate * (1.0 - sig))


def hidden_layer(xa, xb, gate, up, height):
    R, half = xa.shape
    D, Fc = gate.shape
    tile = min(256, Fc)
    row = pl.BlockSpec((height, half), lambda r, f: (r, 0))
    col = pl.BlockSpec((D, tile), lambda r, f: (0, f))
    block = pl.BlockSpec((height, tile), lambda r, f: (r, f))
    return pl.pallas_call(
        hidden_body,
        grid=(R // height, Fc // tile),
        in_specs=[row, row, col, col],
        out_specs=[block] * 3,
        out_shape=[
            jax.ShapeDtypeStruct((R, Fc), BF16),
            jax.ShapeDtypeStruct((R, Fc), F32),
            jax.ShapeDtypeStruct((R, Fc), F32),
        ],
        cost_estimate=LIGHT,
        compiler_params=pltpu.CompilerParams(vmem_limit_bytes=48 << 20),
        name="hidden_layer",
    )(xa, xb, gate, up)


def grads_body(ga_ref, gb_ref, down_ref, silu_ref, fac_ref, hid_ref, up_ref, gate_ref, dots_ref):
    half = ga_ref.shape[1]
    hg = mmt(ga_ref[...], down_ref[:, :half]) + mmt(gb_ref[...], down_ref[:, half:])
    up_ref[...] = (hg * silu_ref[...]).astype(BF16)
    gate_ref[...] = (hg * fac_ref[...]).astype(BF16)
    prod = hg * hid_ref[...].astype(F32)
    lanes = dots_ref.shape[1]
    total = prod[:, :lanes]
    for n in range(1, prod.shape[1] // lanes):
        total = total + prod[:, n * lanes : (n + 1) * lanes]

    @pl.when(pl.program_id(1) == 0)
    def _():
        dots_ref[...] = total

    @pl.when(pl.program_id(1) > 0)
    def _():
        dots_ref[...] += total


def grads(g_a, g_b, down, silu, fac, hidden, height):
    R, Fc = hidden.shape
    half = g_a.shape[1]
    tile = min(256, Fc)
    block = pl.BlockSpec((height, tile), lambda r, f: (r, f))
    return pl.pallas_call(
        grads_body,
        grid=(R // height, Fc // tile),
        in_specs=[
            pl.BlockSpec((height, half), lambda r, f: (r, 0)),
            pl.BlockSpec((height, half), lambda r, f: (r, 0)),
            pl.BlockSpec((tile, 2 * half), lambda r, f: (f, 0)),
            block,
            block,
            block,
        ],
        out_specs=[block, block, pl.BlockSpec((height, 128), lambda r, f: (r, 0))],
        out_shape=[
            jax.ShapeDtypeStruct((R, Fc), BF16),
            jax.ShapeDtypeStruct((R, Fc), BF16),
            jax.ShapeDtypeStruct((R, 128), F32),
        ],
        cost_estimate=LIGHT,
        compiler_params=pltpu.CompilerParams(vmem_limit_bytes=56 << 20),
        name="grads",
    )(g_a, g_b, down, silu, fac, hidden)


def local(tokens, experts_chosen, route_weights, cotangent, gate_weight, up_weight, down_weight):
    E, T, Z = lax.axis_size("expert"), lax.axis_size("tensor"), lax.axis_size("dp")
    me_t, me_d = lax.axis_index("tensor"), lax.axis_index("dp")
    B, Fh = tokens.shape
    K = experts_chosen.shape[1]
    cap = min(B, 9 * B * K // (8 * E) + 1)
    capr = -(-Z * cap // 8) * 8
    G = Z * B
    R = E * capr
    Dq, Ft = gate_weight.shape[1:]
    Fc = Ft // Z
    D = Dq * Z
    two = T == 2 and Z % 2 == 0 and Fh % 256 == 0
    H = R // 2

    def place_of(q):
        if not two:
            return q
        return ((q // (Z // 2)) ^ me_t) * (Z // 2) + q % (Z // 2)

    wide = [experts_chosen.astype(F32)]
    left = route_weights
    for _ in range(3):
        wide.append(left.astype(BF16).astype(F32))
        left = left - wide[-1]
    wide = jnp.concatenate(wide, axis=1).astype(BF16)
    wide = jnp.pad(wide, ((0, 0), (0, 128 - wide.shape[1])))
    tok_g = lax.all_gather(jnp.concatenate([tokens, wide], axis=1), "dp", axis=0, tiled=True)
    cot_g = lax.all_gather(cotangent, "dp", axis=0, tiled=True)

    gate_up_p = [gate_up_chunk(gate_weight[0], up_weight[0], me_d ^ s, Fc) for s in range(Z)]
    down_p = [lax.dynamic_slice_in_dim(down_weight[0], (me_d ^ s) * Fc, Fc, 0) for s in range(Z)]
    tok_g, gate_up_p[3:], down_p = tie(tok_g, gate_up_p[3:], down_p)
    gate_up_p[1] = swap(gate_up_p[1], "dp", 1)
    for s in range(2, Z):
        if s > 2:
            gate_up_p[s], gate_up_p[s - 1] = tie(gate_up_p[s], gate_up_p[s - 1])
        gate_up_p[s] = swap(gate_up_p[s], "dp", s)
    down_p[1], gate_up_p[1] = tie(down_p[1], gate_up_p[1])
    down_p[1] = swap(down_p[1], "dp", 1)
    for s in range(2, Z):
        if s > 2:
            down_p[s], down_p[s - 1] = tie(down_p[s], down_p[s - 1])
        else:
            down_p[s], gate_up_p = tie(down_p[s], gate_up_p)
        down_p[s] = swap(down_p[s], "dp", s)

    routing = tok_g[:, Fh:].astype(F32)
    tok_g = tok_g[:, :Fh]
    ids = routing[:, :K].astype(jnp.int32)
    wts = routing[:, K : 2 * K] + routing[:, 2 * K : 3 * K] + routing[:, 3 * K : 4 * K]
    rel = jnp.arange(E, dtype=jnp.int32)
    named = ids[:, :, None] == rel[None, None, :]
    hit = jnp.any(named, axis=1)
    wtok = jnp.sum(jnp.where(named, wts[:, :, None], 0.0), axis=1)
    order = jnp.arange(G, dtype=jnp.int32)
    before = (order[None, :] < order[:, None]).astype(BF16)
    pos = jnp.where(hit, mm(before, hit.astype(BF16)), -1.0)
    place = pos.T[:, None, :] == jnp.arange(capr, dtype=F32)[None, :, None]
    pick = place.astype(BF16).reshape(R, G)
    heavy = jnp.where(place, wtok.T[:, None, :], 0.0).reshape(R, G)
    heavy_hi = heavy.astype(BF16)
    heavy_lo = (heavy - heavy_hi.astype(F32)).astype(BF16)
    wslot = jnp.sum(heavy, axis=1, keepdims=True)

    def over_expert(rows):
        rows = rows.reshape(E, capr, -1)
        return lax.all_to_all(rows, "expert", 0, 0, tiled=True).reshape(R, -1)

    def widen(half):
        if two:
            return half, swap(half, "tensor", 1)
        full = lax.all_gather(half, "tensor", axis=1, tiled=True)
        return full[:, : D // 2], full[:, D // 2 :]

    if two:
        x_send, g_send = product(pick, tok_g, 0, Fh), product(pick, cot_g, 0, Fh, scale=wslot)
    else:
        x_send, g_send = mm(pick, tok_g).astype(BF16), (mm(pick, cot_g) * wslot).astype(BF16)
    me_e = lax.axis_index("expert")
    x_back = x_send
    for s in range(1, E):
        at = (me_e ^ s) * capr
        part = swap(lax.dynamic_slice_in_dim(x_send, at, capr, 0), "expert", s)
        x_back = lax.dynamic_update_slice_in_dim(x_back, part, at, 0)
    g_send, gate_up_p = tie(g_send, gate_up_p)
    x = widen(x_back)
    g = widen(over_expert(g_send))

    places = place_of(me_d ^ jnp.arange(Z, dtype=jnp.int32))
    gate, up = join(gate_up_p, 0, places, 2)
    hidden, silu, fac = hidden_layer(x[0], x[1], gate, up, H)
    down_p, hidden, silu, fac = lax.optimization_barrier((down_p, hidden, silu, fac))
    (down,) = join(down_p, 1, places, 1)

    def combine(weights, back):
        return lax.dot_general(weights, back, OVER, preferred_element_type=F32)

    def to_blocks(value, dtype):
        def block(s):
            return lax.dynamic_slice_in_dim(value, (me_d ^ s) * B, B, 0)

        total = block(0)
        for s in range(1, Z):
            total = total + swap(block(s).astype(dtype), "dp", s).astype(F32)
        return total

    def fold(make, whole, parts):
        if not two:
            mine = lax.psum_scatter(
                whole().astype(BF16), "tensor", scatter_dimension=1, tiled=True
            )
            return [mine]
        others = [swap(make(parts + n, parts), "tensor", 1) for n in range(parts)]
        return [make(n, parts, others[n]) for n in range(parts)]

    def make_out(first, parts, extra=None):
        return product(hidden, down, first, D // 2 // parts, extra)

    (out_mine,) = fold(make_out, lambda: mm(hidden, down), 1)
    (g_mine, g_other), out_mine = tie(g, out_mine)
    out_back = over_expert(out_mine)
    up_grad, gate_grad, dots = grads(g_mine, g_other, down, silu, fac, hidden, H)

    def make_in(first, parts, extra=None):
        return pair_product(gate_grad, up_grad, gate, up, first, D // 2 // parts, extra)

    in_mine = fold(make_in, lambda: mmt(gate_grad, gate) + mmt(up_grad, up), 2)
    dots = jnp.sum(dots, axis=1)
    if two:
        dots = dots + swap(dots, "tensor", 1)
    else:
        dots = lax.psum(dots, "tensor")
    dots = dots.reshape(E, capr)
    spare = two and capr - Z * cap >= 3 and D // 4 >= capr
    if spare:
        rows3 = []
        for _ in range(3):
            rows3.append(dots.astype(BF16))
            dots = dots - rows3[-1].astype(F32)
        rows3 = jnp.pad(jnp.stack(rows3, axis=1), ((0, 0), (0, 0), (0, D // 4 - capr)))
        last = in_mine[1].reshape(E, capr, -1)
        last = lax.dynamic_update_slice(last, rows3, (0, Z * cap, 0))
        in_mine[1] = last.reshape(R, -1)
    in_mine[0], out_back = tie(in_mine[0], out_back)
    out_tok = (combine(heavy_hi, out_back) + combine(heavy_lo, out_back)).astype(BF16)
    in_back = []
    for n, part in enumerate(in_mine):
        if n:
            part, in_back[n - 1], out_tok = tie(part, in_back[n - 1], out_tok)
        in_back.append(over_expert(part))
    if spare:
        dots = in_back[1].reshape(E, capr, -1)[:, Z * cap : Z * cap + 3, :capr].astype(F32)
        dots = jnp.sum(dots, axis=1)
    else:
        dots = over_expert(dots.reshape(R, 1)).reshape(E, capr)
    layer_output = lax.psum_scatter(out_tok, "dp", scatter_dimension=0, tiled=True)
    token_grad = [to_blocks(combine(pick, p), BF16).astype(BF16) for p in in_back]
    token_grad = jnp.concatenate(token_grad, axis=1)

    by_tok = jnp.sum(jnp.where(place, dots[:, :, None], 0.0), axis=1).T
    by_tok = by_tok / jnp.where(hit, wtok, 1.0)
    pair = jnp.sum(jnp.where(named, by_tok[:, None, :], 0.0), axis=2)
    route_grad = to_blocks(pair, F32)
    return layer_output, token_grad, route_grad


def solution(mesh):
    rows = P(("expert", "dp"), "tensor")
    pairs = P(("expert", "dp"), None)
    wide = P("expert", "dp", "tensor")
    in_specs = (rows, pairs, pairs, rows, wide, wide, P("expert", "tensor", "dp"))
    return jax.shard_map(
        local, mesh=mesh, in_specs=in_specs, out_specs=(rows, rows, pairs), check_vma=False
    )
```

```python
import jax
import jax.numpy as jnp
from jax import lax
from jax.experimental import pallas as pl
from jax.experimental.pallas import tpu as pltpu
from jax.sharding import PartitionSpec as P

F32 = jnp.float32
BF16 = jnp.bfloat16
ROWS = (((1,), (1,)), ((), ()))
OVER = (((0,), (0,)), ((), ()))
LIGHT = pl.CostEstimate(flops=0, bytes_accessed=0, transcendentals=0)


def swap(value, axis, shift):
    size = lax.axis_size(axis)
    return lax.ppermute(value, axis, [(i, i ^ shift) for i in range(size)])


def tie(*values):
    return lax.optimization_barrier(values)


def mm(a, b):
    return jnp.dot(a, b, preferred_element_type=F32)


def mmt(a, b):
    return lax.dot_general(a, b, ROWS, preferred_element_type=F32)


def join_body(at_ref, *refs):
    parts = len(refs) - at_ref.shape[0]
    pieces, wholes = refs[:-parts], refs[-parts:]
    for n, piece in enumerate(pieces):

        @pl.when(pl.program_id(0) == n)
        def _(piece=piece):
            rows = piece.shape[0] // len(wholes)
            for k, whole in enumerate(wholes):
                whole[...] = piece[k * rows : (k + 1) * rows]


def join(pieces, dim, places, parts):
    rows, cols = pieces[0].shape
    rows //= parts
    shape = (rows * len(pieces), cols) if dim == 0 else (rows, cols * len(pieces))
    spec = pl.BlockSpec((rows, cols), lambda n, at: (at[n], 0) if dim == 0 else (0, at[n]))
    return pl.pallas_call(
        join_body,
        grid_spec=pltpu.PrefetchScalarGridSpec(
            num_scalar_prefetch=1,
            grid=(len(pieces),),
            in_specs=[pl.BlockSpec((rows * parts, cols), lambda n, at: (0, 0))] * len(pieces),
            out_specs=[spec] * parts,
        ),
        out_shape=[jax.ShapeDtypeStruct(shape, BF16)] * parts,
        cost_estimate=LIGHT,
        compiler_params=pltpu.CompilerParams(vmem_limit_bytes=56 << 20),
        name="join",
    )(places, *pieces)


def chunk_body(at_ref, gate_ref, up_ref, out_ref):
    @pl.when(pl.program_id(0) == 0)
    def _():
        out_ref[...] = gate_ref[...]

    @pl.when(pl.program_id(0) == 1)
    def _():
        out_ref[...] = up_ref[...]


def gate_up_chunk(gate, up, index, width):
    rows = gate.shape[0]
    tile = rows // 3 if rows % 48 == 0 else rows
    steps = rows // tile
    return pl.pallas_call(
        chunk_body,
        grid_spec=pltpu.PrefetchScalarGridSpec(
            num_scalar_prefetch=1,
            grid=(2, steps),
            in_specs=[
                pl.BlockSpec((tile, width), lambda p, n, at: (jnp.where(p == 0, n, steps - 1), at[0])),
                pl.BlockSpec((tile, width), lambda p, n, at: (jnp.where(p == 0, 0, n), at[0])),
            ],
            out_specs=pl.BlockSpec((tile, width), lambda p, n, at: (p * steps + n, 0)),
        ),
        out_shape=jax.ShapeDtypeStruct((2 * rows, width), BF16),
        cost_estimate=LIGHT,
        name="gate_up_chunk",
    )(jnp.reshape(index, (1,)).astype(jnp.int32), gate, up)


def product_body(a_ref, w_ref, *rest):
    total = mm(a_ref[...], w_ref[...])
    if len(rest) == 2 and rest[0].shape[1] == 1:
        total = total * rest[0][...]
    elif len(rest) == 2:
        total = total + rest[0][...].astype(F32)
    rest[-1][...] = total.astype(BF16)


def product(a, w, first, width, extra=None, scale=None):
    height, depth = a.shape
    tile = 512 if width % 512 == 0 else 256
    steps = width // tile
    out_spec = pl.BlockSpec((height, tile), lambda n: (0, n))
    return pl.pallas_call(
        product_body,
        grid=(steps,),
        in_specs=[
            pl.BlockSpec((height, depth), lambda n: (0, 0)),
            pl.BlockSpec((depth, tile), lambda n: (0, first * steps + n)),
        ]
        + ([] if extra is None else [out_spec])
        + ([] if scale is None else [pl.BlockSpec((height, 1), lambda n: (0, 0))]),
        out_specs=out_spec,
        out_shape=jax.ShapeDtypeStruct((height, width), BF16),
        cost_estimate=LIGHT,
        compiler_params=pltpu.CompilerParams(vmem_limit_bytes=56 << 20),
        name="product",
    )(*([a, w] + [part for part in (extra, scale) if part is not None]))


def pair_body(a_ref, b_ref, wa_ref, wb_ref, *rest):
    total = mmt(a_ref[...], wa_ref[...]) + mmt(b_ref[...], wb_ref[...])
    if len(rest) == 2:
        total = total + rest[0][...].astype(F32)
    rest[-1][...] = total.astype(BF16)


def pair_product(a, b, wa, wb, first, width, extra=None):
    height, depth = a.shape
    tile = 256
    steps = width // tile
    row_spec = pl.BlockSpec((height, depth), lambda n: (0, 0))
    col_spec = pl.BlockSpec((tile, depth), lambda n: (first * steps + n, 0))
    out_spec = pl.BlockSpec((height, tile), lambda n: (0, n))
    ins = [a, b, wa, wb] + ([] if extra is None else [extra])
    return pl.pallas_call(
        pair_body,
        grid=(steps,),
        in_specs=[row_spec, row_spec, col_spec, col_spec] + ([] if extra is None else [out_spec]),
        out_specs=out_spec,
        out_shape=jax.ShapeDtypeStruct((height, width), BF16),
        cost_estimate=LIGHT,
        compiler_params=pltpu.CompilerParams(vmem_limit_bytes=56 << 20),
        name="pair_product",
    )(*ins)


def hidden_body(xa_ref, xb_ref, gate_ref, up_ref, hid_ref, silu_ref, fac_ref):
    half = xa_ref.shape[1]

    def pre(w_ref):
        return mm(xa_ref[...], w_ref[:half]) + mm(xb_ref[...], w_ref[half:])

    gate, up = pre(gate_ref), pre(up_ref)
    sig = jax.nn.sigmoid(gate)
    silu = gate * sig
    silu_ref[...] = silu
    hid_ref[...] = (silu * up).astype(BF16)
    fac_ref[...] = up * sig * (1.0 + gate * (1.0 - sig))


def hidden_layer(xa, xb, gate, up, height):
    R, half = xa.shape
    D, Fc = gate.shape
    tile = min(256, Fc)
    row = pl.BlockSpec((height, half), lambda r, f: (r, 0))
    col = pl.BlockSpec((D, tile), lambda r, f: (0, f))
    block = pl.BlockSpec((height, tile), lambda r, f: (r, f))
    return pl.pallas_call(
        hidden_body,
        grid=(R // height, Fc // tile),
        in_specs=[row, row, col, col],
        out_specs=[block] * 3,
        out_shape=[
            jax.ShapeDtypeStruct((R, Fc), BF16),
            jax.ShapeDtypeStruct((R, Fc), F32),
            jax.ShapeDtypeStruct((R, Fc), F32),
        ],
        cost_estimate=LIGHT,
        compiler_params=pltpu.CompilerParams(vmem_limit_bytes=48 << 20),
        name="hidden_layer",
    )(xa, xb, gate, up)


def grads_body(ga_ref, gb_ref, down_ref, silu_ref, fac_ref, hid_ref, up_ref, gate_ref, dots_ref):
    half = ga_ref.shape[1]
    hg = mmt(ga_ref[...], down_ref[:, :half]) + mmt(gb_ref[...], down_ref[:, half:])
    up_ref[...] = (hg * silu_ref[...]).astype(BF16)
    gate_ref[...] = (hg * fac_ref[...]).astype(BF16)
    prod = hg * hid_ref[...].astype(F32)
    lanes = dots_ref.shape[1]
    total = prod[:, :lanes]
    for n in range(1, prod.shape[1] // lanes):
        total = total + prod[:, n * lanes : (n + 1) * lanes]

    @pl.when(pl.program_id(1) == 0)
    def _():
        dots_ref[...] = total

    @pl.when(pl.program_id(1) > 0)
    def _():
        dots_ref[...] += total


def grads(g_a, g_b, down, silu, fac, hidden, height):
    R, Fc = hidden.shape
    half = g_a.shape[1]
    tile = min(256, Fc)
    block = pl.BlockSpec((height, tile), lambda r, f: (r, f))
    return pl.pallas_call(
        grads_body,
        grid=(R // height, Fc // tile),
        in_specs=[
            pl.BlockSpec((height, half), lambda r, f: (r, 0)),
            pl.BlockSpec((height, half), lambda r, f: (r, 0)),
            pl.BlockSpec((tile, 2 * half), lambda r, f: (f, 0)),
            block,
            block,
            block,
        ],
        out_specs=[block, block, pl.BlockSpec((height, 128), lambda r, f: (r, 0))],
        out_shape=[
            jax.ShapeDtypeStruct((R, Fc), BF16),
            jax.ShapeDtypeStruct((R, Fc), BF16),
            jax.ShapeDtypeStruct((R, 128), F32),
        ],
        cost_estimate=LIGHT,
        compiler_params=pltpu.CompilerParams(vmem_limit_bytes=56 << 20),
        name="grads",
    )(g_a, g_b, down, silu, fac, hidden)


def local(tokens, experts_chosen, route_weights, cotangent, gate_weight, up_weight, down_weight):
    E, T, Z = lax.axis_size("expert"), lax.axis_size("tensor"), lax.axis_size("dp")
    me_t, me_d = lax.axis_index("tensor"), lax.axis_index("dp")
    B, Fh = tokens.shape
    K = experts_chosen.shape[1]
    cap = min(B, 9 * B * K // (8 * E) + 1)
    capr = -(-Z * cap // 8) * 8
    G = Z * B
    R = E * capr
    Dq, Ft = gate_weight.shape[1:]
    Fc = Ft // Z
    D = Dq * Z
    two = T == 2 and Z % 2 == 0 and Fh % 256 == 0
    H = R // 2

    def place_of(q):
        if not two:
            return q
        return ((q // (Z // 2)) ^ me_t) * (Z // 2) + q % (Z // 2)

    wide = [experts_chosen.astype(F32)]
    left = route_weights
    for _ in range(3):
        wide.append(left.astype(BF16).astype(F32))
        left = left - wide[-1]
    wide = jnp.concatenate(wide, axis=1).astype(BF16)
    wide = jnp.pad(wide, ((0, 0), (0, 128 - wide.shape[1])))
    tok_g = lax.all_gather(jnp.concatenate([tokens, wide], axis=1), "dp", axis=0, tiled=True)
    cot_g = lax.all_gather(cotangent, "dp", axis=0, tiled=True)

    gate_up_p = [gate_up_chunk(gate_weight[0], up_weight[0], me_d ^ s, Fc) for s in range(Z)]
    down_p = [lax.dynamic_slice_in_dim(down_weight[0], (me_d ^ s) * Fc, Fc, 0) for s in range(Z)]
    tok_g, gate_up_p[3:], down_p = tie(tok_g, gate_up_p[3:], down_p)
    gate_up_p[1] = swap(gate_up_p[1], "dp", 1)
    for s in range(2, Z):
        if s > 2:
            gate_up_p[s], gate_up_p[s - 1] = tie(gate_up_p[s], gate_up_p[s - 1])
        gate_up_p[s] = swap(gate_up_p[s], "dp", s)
    down_p[1], gate_up_p[1] = tie(down_p[1], gate_up_p[1])
    down_p[1] = swap(down_p[1], "dp", 1)
    for s in range(2, Z):
        if s > 2:
            down_p[s], down_p[s - 1] = tie(down_p[s], down_p[s - 1])
        else:
            down_p[s], gate_up_p = tie(down_p[s], gate_up_p)
        down_p[s] = swap(down_p[s], "dp", s)

    routing = tok_g[:, Fh:].astype(F32)
    tok_g = tok_g[:, :Fh]
    ids = routing[:, :K].astype(jnp.int32)
    wts = routing[:, K : 2 * K] + routing[:, 2 * K : 3 * K] + routing[:, 3 * K : 4 * K]
    rel = jnp.arange(E, dtype=jnp.int32)
    named = ids[:, :, None] == rel[None, None, :]
    hit = jnp.any(named, axis=1)
    wtok = jnp.sum(jnp.where(named, wts[:, :, None], 0.0), axis=1)
    order = jnp.arange(G, dtype=jnp.int32)
    before = (order[None, :] < order[:, None]).astype(BF16)
    pos = jnp.where(hit, mm(before, hit.astype(BF16)), -1.0)
    place = pos.T[:, None, :] == jnp.arange(capr, dtype=F32)[None, :, None]
    pick = place.astype(BF16).reshape(R, G)
    heavy = jnp.where(place, wtok.T[:, None, :], 0.0).reshape(R, G)
    heavy_hi = heavy.astype(BF16)
    heavy_lo = (heavy - heavy_hi.astype(F32)).astype(BF16)
    wslot = jnp.sum(heavy, axis=1, keepdims=True)

    def over_expert(rows):
        rows = rows.reshape(E, capr, -1)
        return lax.all_to_all(rows, "expert", 0, 0, tiled=True).reshape(R, -1)

    def widen(half):
        if two:
            return half, swap(half, "tensor", 1)
        full = lax.all_gather(half, "tensor", axis=1, tiled=True)
        return full[:, : D // 2], full[:, D // 2 :]

    if two:
        x_send, g_send = product(pick, tok_g, 0, Fh), product(pick, cot_g, 0, Fh, scale=wslot)
    else:
        x_send, g_send = mm(pick, tok_g).astype(BF16), (mm(pick, cot_g) * wslot).astype(BF16)
    me_e = lax.axis_index("expert")
    x_back = x_send
    for s in range(1, E):
        at = (me_e ^ s) * capr
        part = swap(lax.dynamic_slice_in_dim(x_send, at, capr, 0), "expert", s)
        x_back = lax.dynamic_update_slice_in_dim(x_back, part, at, 0)
    g_send, gate_up_p = tie(g_send, gate_up_p)
    x = widen(x_back)
    g = widen(over_expert(g_send))

    places = place_of(me_d ^ jnp.arange(Z, dtype=jnp.int32))
    gate, up = join(gate_up_p, 0, places, 2)
    hidden, silu, fac = hidden_layer(x[0], x[1], gate, up, H)
    down_p, hidden, silu, fac = lax.optimization_barrier((down_p, hidden, silu, fac))
    (down,) = join(down_p, 1, places, 1)

    def combine(weights, back):
        return lax.dot_general(weights, back, OVER, preferred_element_type=F32)

    def to_blocks(value, dtype):
        def block(s):
            return lax.dynamic_slice_in_dim(value, (me_d ^ s) * B, B, 0)

        total = block(0)
        for s in range(1, Z):
            total = total + swap(block(s).astype(dtype), "dp", s).astype(F32)
        return total

    def fold(make, whole, parts):
        if not two:
            mine = lax.psum_scatter(
                whole().astype(BF16), "tensor", scatter_dimension=1, tiled=True
            )
            return [mine]
        others = [swap(make(parts + n, parts), "tensor", 1) for n in range(parts)]
        return [make(n, parts, others[n]) for n in range(parts)]

    def make_out(first, parts, extra=None):
        return product(hidden, down, first, D // 2 // parts, extra)

    (out_mine,) = fold(make_out, lambda: mm(hidden, down), 1)
    (g_mine, g_other), out_mine = tie(g, out_mine)
    out_back = over_expert(out_mine)
    up_grad, gate_grad, dots = grads(g_mine, g_other, down, silu, fac, hidden, H)

    def make_in(first, parts, extra=None):
        return pair_product(gate_grad, up_grad, gate, up, first, D // 2 // parts, extra)

    in_mine = fold(make_in, lambda: mmt(gate_grad, gate) + mmt(up_grad, up), 2)
    dots = jnp.sum(dots, axis=1)
    if two:
        dots = dots + swap(dots, "tensor", 1)
    else:
        dots = lax.psum(dots, "tensor")
    dots = dots.reshape(E, capr)
    spare = two and capr - Z * cap >= 3 and D // 4 >= capr
    if spare:
        rows3 = []
        for _ in range(3):
            rows3.append(dots.astype(BF16))
            dots = dots - rows3[-1].astype(F32)
        rows3 = jnp.pad(jnp.stack(rows3, axis=1), ((0, 0), (0, 0), (0, D // 4 - capr)))
        last = in_mine[1].reshape(E, capr, -1)
        last = lax.dynamic_update_slice(last, rows3, (0, Z * cap, 0))
        in_mine[1] = last.reshape(R, -1)
    in_mine[0], out_back = tie(in_mine[0], out_back)
    out_tok = (combine(heavy_hi, out_back) + combine(heavy_lo, out_back)).astype(BF16)
    in_back = []
    for n, part in enumerate(in_mine):
        if n:
            part, in_back[n - 1], out_tok = tie(part, in_back[n - 1], out_tok)
        in_back.append(over_expert(part))
    if spare:
        dots = in_back[1].reshape(E, capr, -1)[:, Z * cap : Z * cap + 3, :capr].astype(F32)
        dots = jnp.sum(dots, axis=1)
    else:
        dots = over_expert(dots.reshape(R, 1)).reshape(E, capr)
    layer_output = lax.psum_scatter(out_tok, "dp", scatter_dimension=0, tiled=True)
    token_grad = [to_blocks(combine(pick, p), BF16).astype(BF16) for p in in_back]
    token_grad = jnp.concatenate(token_grad, axis=1)

    by_tok = jnp.sum(jnp.where(place, dots[:, :, None], 0.0), axis=1).T
    by_tok = by_tok / jnp.where(hit, wtok, 1.0)
    pair = jnp.sum(jnp.where(named, by_tok[:, None, :], 0.0), axis=2)
    route_grad = to_blocks(pair, F32)
    return layer_output, token_grad, route_grad


def solution(mesh):
    rows = P(("expert", "dp"), "tensor")
    pairs = P(("expert", "dp"), None)
    wide = P("expert", "dp", "tensor")
    in_specs = (rows, pairs, pairs, rows, wide, wide, P("expert", "tensor", "dp"))
    return jax.shard_map(
        local, mesh=mesh, in_specs=in_specs, out_specs=(rows, rows, pairs), check_vma=False
    )
```
